32 devices in a mesh: wide: 8 (over z, x), narrow: 4 (over y, core).
Axes of the slice: x: 2, y: 2, z: 4, core: 2. Of those that a mesh axis runs over, the one named last changes fastest.
Arguments:
- pressure: float32 [1024, 128], P(('wide', 'narrow')), may hold values from -6 to 6
- right_side: float32 [1024, 128], P(('wide', 'narrow')), may hold values from -6 to 6
- concentration: float32 [1024, 128], P(('wide', 'narrow')), may hold values from 0 to 1
- pore_volume: float32 [1024, 128], P(('wide', 'narrow')), may hold values from 0.5 to 2
- well_rate: float32 [1024, 128], P(('wide', 'narrow')), may hold values from 0.02 to 0.5
- inject_conc: float32 [1024, 128], P(('wide', 'narrow')), may hold values from 0 to 1
- transmissibility: float32 [6, 131072], P(None, ('wide', 'narrow')), may hold values from 0.1 to 1
- face_neighbor: int32 [6, 1024], P(None, ('wide', 'narrow')), may hold values from 0 to 56, as said below
- sub_matrix: bfloat16 [2048, 4, 128, 128], P(('wide', 'narrow')), as said below
- sub_columns: int32 [2048, 4], P(('wide', 'narrow')), may hold values from 0 to 63, as said below
- send_blocks: int32 [32, 4, 8], P(('wide', 'narrow')), may hold values from 0 to 31, as said below
- send_counts: int32 [32, 4], P(('wide', 'narrow')), may hold values from 1 to 8, as said below
- basis_weights: bfloat16 [8192, 4096], P(('wide', 'narrow')), may hold values from -0.09375 to 0.09375
- coarse_index: int32 [8192], P(('wide', 'narrow')), may hold values from 0 to 4095, as said below
- coarse_inverse: float32 [4096, 512], P(('wide', 'narrow')), may hold values from -0.25 to 0.25
Outputs:
- pressure_new: float32 [1024, 128], P(('wide', 'narrow'))
- concentration_new: float32 [1024, 128], P(('wide', 'narrow'))
The draws below stay inside these ranges and needn't reach their ends.
Inputs may be any that keep to these rules, and one draw needn't show every extreme that they name: `send_blocks`: local block indices below 32. `send_counts`: between 1 and 8; the first subdomain sends 8 blocks to every neighbour and the last sends one. `sub_columns`: slot 0 of each row block names the row block itself. `face_neighbor`: each owned block's faces name owned blocks or the first received block from some neighbour. `coarse_index`: a subdomain's functions may be owned by any index of wide, and may repeat. `sub_matrix`: the diagonal of each row block's first stored block lies between 0.9 and 2.1.
All inputs are finite; a program needn't handle non-finite values.
Results may differ from the reference program's by a relative error of at most 0.00225.
The reference program's roundings to bfloat16 on the way (of `pressure_b`, `residual_b` and `coarse_b`) count: a program that leaves them out, or rounds other values in their place, can miss the bound.
Values may be sent and summed in bfloat16 or wider, within the bound.
A program may use at most 64 MiB of HBM per device.

```python
import math
import jax
import jax.numpy as jnp
from jax import lax

BS = 128
BD = 32
SL = 8
EXT = 64
EROWS = 2048
NNZB = 4
SWEEPS = 4
NFACE = 6
NCL = 256
NCO = 512
NC = 4096
BLOCKS = 1024
CELLS = 131072
N_WIDE = 8
N_NARROW = 4
DEVICES = 32


def draw_sub_matrix(key, part):
    noise_key, diag_key = jax.random.split(key)
    noise = jax.random.normal(noise_key, (EROWS, NNZB, BS, BS), jnp.float32) * (0.3 / math.sqrt(NNZB * BS))
    diag_values = jax.random.uniform(diag_key, (EROWS, 1, BS, 1), jnp.float32, 1.0, 2.0)
    first_slot = (jnp.arange(NNZB) == 0).astype(jnp.float32)[None, :, None, None]
    identity = jnp.eye(BS, dtype=jnp.float32)[None, None]
    return (noise + first_slot * identity * diag_values).astype(jnp.bfloat16)


def draw_sub_columns(key, part):
    own_rows = (jnp.arange(EROWS, dtype=jnp.int32) % EXT)[:, None]
    others = jax.random.randint(key, (EROWS, NNZB - 1), 0, EXT, dtype=jnp.int32)
    return jnp.concatenate([own_rows, others], axis=1)


def draw_send_blocks(key, part):
    return jax.random.randint(key, (DEVICES, 4, SL), 0, BD, dtype=jnp.int32)


def draw_send_counts(key, part):
    counts = jax.random.randint(key, (DEVICES, 4), 1, SL + 1, dtype=jnp.int32)
    counts = counts.at[0].set(SL)
    return counts.at[DEVICES - 1].set(1)


def draw_coarse_index(key, part):
    return jax.random.randint(key, (DEVICES * NCL,), 0, NC, dtype=jnp.int32)


def draw_face_neighbor(key, part):
    first_key, second_key = jax.random.split(key)
    block_local = jnp.arange(BLOCKS, dtype=jnp.int32) % BD
    turn = jax.random.randint(first_key, (), 0, 4, dtype=jnp.int32)
    direction = (jnp.arange(BLOCKS, dtype=jnp.int32) + turn) % 4
    margin_block = BD + direction * SL
    random_block = jax.random.randint(second_key, (BLOCKS,), 0, BD, dtype=jnp.int32)
    return jnp.stack([(block_local + 1) % BD, (block_local - 1) % BD, (block_local + 2) % BD, (block_local - 2) % BD, margin_block, random_block], axis=0)


def levels(own_key, dims, shards, least, top_value):
    loudness, own = 1.0, jax.random.fold_in(own_key, 6)
    for axis_at, parts in shards:
        steps = jnp.exp(jax.random.uniform(jax.random.fold_in(own, axis_at), (parts,), jnp.float32, least / len(shards), top_value / len(shards)))
        loudness = loudness * jnp.repeat(steps, dims[axis_at] // parts).reshape([-1 if axis == axis_at else 1 for axis in range(len(dims))])
    return loudness


def centred(rng, extent, scale, reach, cuts=(), kind=jnp.bfloat16):
    level = levels(rng, extent, cuts, -0.22, 0.18) if cuts else 1.0
    entries = jax.random.normal(rng, extent, jnp.float32) * scale * level
    return jnp.minimum(jnp.maximum(entries, -reach), reach).astype(kind)


def setup_inputs(seed: int = 0) -> dict:
    streams_of = jax.random.split(jax.random.key(seed), 16)
    pressure = centred(streams_of[0], (BLOCKS, BS), 1.0, 6.0, ((0, 32),), jnp.float32)
    right_side = centred(streams_of[1], (BLOCKS, BS), 1.0, 6.0, ((0, 32),), jnp.float32)
    concentration = jnp.clip(1.0 * jax.random.uniform(streams_of[2], (BLOCKS, BS), jnp.float32) ** levels(streams_of[2], (BLOCKS, BS), ((0, 32),), -0.2, 0.2), 0.0, 1.0)
    pore_volume = jnp.clip(jnp.exp(math.log(2.0) - 1.3862944 * jax.random.uniform(streams_of[3], (BLOCKS, BS), jnp.float32) ** levels(streams_of[3], (BLOCKS, BS), ((0, 32),), -0.2, 0.2)), 0.5, 2.0)
    well_rate = jnp.clip(jnp.exp(math.log(0.5) - 3.218876 * jax.random.uniform(streams_of[4], (BLOCKS, BS), jnp.float32) ** levels(streams_of[4], (BLOCKS, BS), ((0, 32),), -0.2, 0.2)), 0.02, 0.5)
    inject_conc = jnp.clip(1.0 * jax.random.uniform(streams_of[5], (BLOCKS, BS), jnp.float32) ** levels(streams_of[5], (BLOCKS, BS), ((0, 32),), -0.2, 0.2), 0.0, 1.0)
    transmissibility = jnp.clip(jnp.exp(math.log(1.0) - 2.3025851 * jax.random.uniform(streams_of[6], (NFACE, CELLS), jnp.float32) ** levels(streams_of[6], (NFACE, CELLS), ((1, 32),), -0.2, 0.2)), 0.1, 1.0)
    face_neighbor = draw_face_neighbor(jax.random.fold_in(streams_of[15], 71), 0)
    sub_matrix = draw_sub_matrix(jax.random.fold_in(streams_of[15], 71), 0)
    sub_columns = draw_sub_columns(jax.random.fold_in(streams_of[15], 71), 0)
    send_blocks = draw_send_blocks(jax.random.fold_in(streams_of[15], 71), 0)
    send_counts = draw_send_counts(jax.random.fold_in(streams_of[15], 71), 0)
    basis_weights = centred(streams_of[12], (DEVICES * NCL, BD * BS), (BD * BS) ** -0.5, 0.09375, ((0, 32),))
    coarse_index = draw_coarse_index(jax.random.fold_in(streams_of[15], 71), 0)
    coarse_inverse = centred(streams_of[14], (NC, NCO), NCO ** -0.5, 0.25, ((0, 32),), jnp.float32)
    return dict(pressure=pressure, right_side=right_side, concentration=concentration, pore_volume=pore_volume, well_rate=well_rate, inject_conc=inject_conc, transmissibility=transmissibility, face_neighbor=face_neighbor, sub_matrix=sub_matrix, sub_columns=sub_columns, send_blocks=send_blocks, send_counts=send_counts, basis_weights=basis_weights, coarse_index=coarse_index, coarse_inverse=coarse_inverse)


shift_offsets = (2, 1, -1, -2)
courant = 0.9


def product_ref(matrix, columns, vector_b):
    vector_b = lax.optimization_barrier(vector_b)
    picked = vector_b[columns].astype(jnp.float32)
    return jnp.einsum("rkij,rkj->ri", matrix.astype(jnp.float32), picked)


def outgoing(owned_rows, send_blocks, send_counts):
    slot_count = send_blocks.shape[-1]
    active = jnp.arange(slot_count)[None, None, :] < send_counts[:, :, None]
    picked = jax.vmap(lambda block_rows, chosen: block_rows[chosen])(owned_rows, send_blocks)
    return jnp.where(active[..., None], picked, jnp.zeros_like(picked))


def extended(owned_rows, send_blocks, send_counts, wide_count):
    packed = outgoing(owned_rows, send_blocks, send_counts)
    devices = owned_rows.shape[0]
    narrow_count = devices // wide_count
    slot_count = send_blocks.shape[-1]
    grid = packed.reshape((wide_count, narrow_count) + packed.shape[1:])
    collected = [owned_rows]
    for position, offset in enumerate(shift_offsets):
        source = grid[:, :, position]
        zero_rows = jnp.zeros((abs(offset),) + source.shape[1:], source.dtype)
        if offset > 0:
            moved_rows = jnp.concatenate([zero_rows, source[:wide_count - offset]], axis=0)
        else:
            moved_rows = jnp.concatenate([source[-offset:], zero_rows], axis=0)
        collected.append(moved_rows.reshape((devices, slot_count) + source.shape[3:]))
    return jnp.concatenate(collected, axis=1)


def reference(pressure, right_side, concentration, pore_volume, well_rate, inject_conc, transmissibility, face_neighbor, sub_matrix, sub_columns, send_blocks, send_counts, basis_weights, coarse_index, coarse_inverse):
    wide_count = N_WIDE
    devices = N_WIDE * N_NARROW
    cells_dev = BD * BS
    pressure_dev = pressure.reshape(devices, BD, BS)
    right_dev = right_side.reshape(devices, BD, BS)
    conc_dev = concentration.reshape(devices, BD, BS)
    matrix_dev = sub_matrix.reshape(devices, EXT, NNZB, BS, BS)
    columns_dev = sub_columns.reshape(devices, EXT, NNZB)
    pressure_b = pressure_dev.astype(jnp.bfloat16)
    ext_pressure = extended(pressure_b, send_blocks, send_counts, wide_count)

    def residual_one(members):
        matrix, columns, ext_vector, right_rows = members
        return right_rows - product_ref(matrix[:BD], columns[:BD], ext_vector)

    residual = lax.map(residual_one, (matrix_dev, columns_dev, ext_pressure, right_dev))
    residual_b = residual.astype(jnp.bfloat16)
    ext_residual = extended(residual_b, send_blocks, send_counts, wide_count)

    def smooth_one(members):
        matrix, columns, ext_vector = members
        diagonal = jnp.diagonal(matrix[:, 0], axis1=1, axis2=2).astype(jnp.float32)
        target = ext_vector.astype(jnp.float32)
        update = jnp.zeros(target.shape, jnp.float32)
        for turn_index in range(SWEEPS):
            update = update + (target - product_ref(matrix, columns, update.astype(jnp.bfloat16))) / diagonal
        return update[:BD]

    local_update = lax.map(smooth_one, (matrix_dev, columns_dev, ext_residual))
    basis_dev = basis_weights.reshape(devices, NCL, cells_dev)
    local_coarse = lax.map(lambda members: jnp.dot(members[0], members[1].reshape(-1), preferred_element_type=jnp.float32), (basis_dev, residual_b))
    coarse_residual = jnp.zeros((NC,), jnp.float32).at[coarse_index].add(local_coarse.reshape(-1))
    inverse_blocks = coarse_inverse.reshape(N_WIDE, NCO, NCO)
    coarse_values = jnp.einsum("wij,wj->wi", inverse_blocks, coarse_residual.reshape(N_WIDE, NCO), precision=lax.Precision.HIGHEST).reshape(-1)
    coarse_b = coarse_values.astype(jnp.bfloat16)
    index_dev = coarse_index.reshape(devices, NCL)
    correction = lax.map(lambda members: jnp.dot(coarse_b[members[1]], members[0], preferred_element_type=jnp.float32), (basis_dev, index_dev))
    pressure_next = pressure_dev + local_update + correction.reshape(devices, BD, BS)
    ext_next = extended(pressure_next, send_blocks, send_counts, wide_count)
    ext_conc = extended(conc_dev, send_blocks, send_counts, wide_count)
    neighbor_dev = face_neighbor.reshape(NFACE, devices, BD).transpose(1, 0, 2)
    trans_dev = transmissibility.reshape(NFACE, devices, cells_dev).transpose(1, 0, 2)
    near_pressure = jax.vmap(lambda values, where_to: values[where_to])(ext_next, neighbor_dev).reshape(devices, NFACE, cells_dev)
    near_conc = jax.vmap(lambda values, where_to: values[where_to])(ext_conc, neighbor_dev).reshape(devices, NFACE, cells_dev)
    own_pressure = pressure_next.reshape(devices, 1, cells_dev)
    own_conc = conc_dev.reshape(devices, 1, cells_dev)
    face_flux = trans_dev * (own_pressure - near_pressure)
    outward = jnp.maximum(face_flux, 0.0)
    inward = jnp.minimum(face_flux, 0.0)
    advection = jnp.sum(outward * own_conc + inward * near_conc, axis=1)
    outflow = jnp.sum(outward, axis=1)
    volume_flat = pore_volume.reshape(devices, cells_dev)
    rate_flat = well_rate.reshape(devices, cells_dev)
    cell_rate = (outflow + rate_flat) / volume_flat
    time_step = courant / jnp.max(cell_rate)
    conc_flat = conc_dev.reshape(devices, cells_dev)
    inject_flat = inject_conc.reshape(devices, cells_dev)
    conc_next = conc_flat + time_step / volume_flat * (rate_flat * (inject_flat - conc_flat) - advection)
    return pressure_next.reshape(BLOCKS, BS), conc_next.reshape(BLOCKS, BS)
```

```python
import functools

import jax
import jax.numpy as jnp
from jax import lax
from jax.experimental import pallas as pl
from jax.experimental.pallas import tpu as pltpu
from jax.sharding import PartitionSpec as P

SWEEPS = 4

shift_offsets = (2, 1, -1, -2)
courant = 0.9
MESH = pl.DeviceIdType.MESH
f32, bf16 = jnp.float32, jnp.bfloat16
contract_last = (((1,), (1,)), ((), ()))
plain = (((1,), (0,)), ((), ()))


def rounded(value):
    return value.astype(bf16).astype(f32)


def kernel(
    wide_count,
    narrow_count,
    face_neighbor,
    sub_columns,
    send_blocks,
    send_counts,
    index_column,
    pressure_hbm,
    right_hbm,
    conc_hbm,
    volume_hbm,
    rate_hbm,
    inject_hbm,
    trans_hbm,
    matrix_hbm,
    basis_hbm,
    inverse_hbm,
    pressure_out,
    conc_out,
    pressure,
    right_side,
    conc,
    volume,
    rate,
    inject,
    trans,
    matrix,
    basis,
    inverse,
    load_sem,
    outbox,
    inbox,
    margin_send,
    margin_recv,
    own,
    ext_a,
    ext_b,
    target,
    diag,
    picked,
    onehot,
    partial,
    wide_in,
    wide_sum,
    narrow_in,
    value_in,
    value_mine,
    coarse_in,
    coarse_mine,
    top_mine,
    top_narrow,
    top_half,
    top_wide,
    wide_send,
    wide_recv,
    narrow_send,
    narrow_recv,
    near_p,
    near_c,
    ext_c,
    adv,
):
    w, n = lax.axis_index("wide"), lax.axis_index("narrow")
    owned, lanes = pressure.shape
    extent = ext_a.shape[0]
    slots = outbox.shape[2]
    faces = trans.shape[0]
    coarse_width = inverse.shape[1]

    loads = []
    sources = (
        (pressure_hbm, pressure),
        (conc_hbm, conc),
        (matrix_hbm.at[pl.ds(0, owned)], matrix.at[pl.ds(0, owned)]),
        (matrix_hbm.at[pl.ds(owned, extent - owned)], matrix.at[pl.ds(owned, extent - owned)]),
        (right_hbm, right_side),
        (basis_hbm, basis),
        (inverse_hbm, inverse),
        (trans_hbm, trans),
        (volume_hbm, volume),
        (rate_hbm, rate),
        (inject_hbm, inject),
    )
    for at, (source, place) in enumerate(sources):
        copy = pltpu.make_async_copy(source, place, load_sem.at[at])
        copy.start()
        loads.append(copy)

    barrier = pltpu.get_barrier_semaphore()
    for step in range(1, wide_count):
        pl.semaphore_signal(barrier, inc=1, device_id=(lax.rem(w + step, wide_count), n), device_id_type=MESH)
    for step in range(1, narrow_count):
        pl.semaphore_signal(barrier, inc=1, device_id=(w, lax.rem(n + step, narrow_count)), device_id_type=MESH)

    def margin_copy(turn, position):
        offset = shift_offsets[position]
        return pltpu.make_async_remote_copy(
            src_ref=outbox.at[turn, position],
            dst_ref=inbox.at[turn, position],
            send_sem=margin_send.at[turn, position],
            recv_sem=margin_recv.at[turn, position],
            device_id=(w + offset, n),
            device_id_type=MESH,
        )

    def reaches(offset):
        return jnp.logical_and(w + offset >= 0, w + offset < wide_count)

    slot_id = lax.broadcasted_iota(jnp.int32, (slots, lanes), 0)

    def pack(turn, rows):
        for position in range(4):
            for t in range(slots):
                outbox[turn, position, pl.ds(t, 1), :] = rows[pl.ds(send_blocks[0, position, t], 1), :]
            filled = outbox[turn, position]
            outbox[turn, position] = jnp.where(slot_id < send_counts[0, position], filled, 0.0)

    def send_margin(turn):
        for position, offset in enumerate(shift_offsets):
            @pl.when(reaches(offset))
            def _():
                margin_copy(turn, position).start()

    def take_margin(turn, place):
        for position, offset in enumerate(shift_offsets):
            rows = pl.ds(owned + position * slots, slots)

            @pl.when(reaches(-offset))
            def _():
                margin_copy(turn, position).wait_recv()
                place[rows, :] = inbox[turn, position]

            @pl.when(jnp.logical_not(reaches(-offset)))
            def _():
                place[rows, :] = jnp.zeros((slots, lanes), f32)

    def exchange(turn, axis, send_from, land_in):
        is_wide = axis == "wide"
        count = wide_count if is_wide else narrow_count
        me = w if is_wide else n
        sends, recvs = (wide_send, wide_recv) if is_wide else (narrow_send, narrow_recv)

        def describe(peer, slot):
            return pltpu.make_async_remote_copy(
                src_ref=send_from(peer),
                dst_ref=land_in.at[slot],
                send_sem=sends.at[turn, peer],
                recv_sem=recvs.at[turn, slot],
                device_id=(peer, n) if is_wide else (w, peer),
                device_id_type=MESH,
            )

        def start():
            @pl.loop(1, count)
            def _(step):
                describe(lax.rem(me + step, count), me).start()

        def take():
            @pl.loop(1, count)
            def _(step):
                peer = lax.rem(me + step, count)
                describe(peer, peer).wait_recv()

        def finish():
            @pl.loop(1, count)
            def _(step):
                describe(lax.rem(me + step, count), me).wait_send()

        return start, take, finish

    residual_wide = exchange(0, "wide", lambda peer: partial.at[peer], wide_in)
    residual_narrow = exchange(0, "narrow", lambda peer: wide_sum, narrow_in)
    values_narrow = exchange(1, "narrow", lambda peer: value_mine, value_in)
    values_wide = exchange(1, "wide", lambda peer: coarse_mine, coarse_in)
    tops_narrow = exchange(2, "narrow", lambda peer: top_mine, top_narrow)
    tops_wide = exchange(2, "wide", lambda peer: top_half, top_wide)

    loads[0].wait()
    own[...] = rounded(pressure[...])
    pack(0, own)
    loads[1].wait()
    pack(1, conc)
    pl.semaphore_wait(barrier, wide_count + narrow_count - 2)
    send_margin(0)
    send_margin(1)

    @pl.loop(0, onehot.shape[1] // lanes)
    def _(chunk):
        numbers = lax.broadcasted_iota(jnp.int32, (onehot.shape[0], lanes), 1) + chunk * lanes
        hit = jnp.where(index_column[...] == numbers, 1.0, 0.0)
        onehot[:, pl.ds(pl.multiple_of(chunk * lanes, lanes), lanes)] = hit.astype(bf16)

    loads[2].wait()
    loads[3].wait()
    eye = lax.broadcasted_iota(jnp.int32, (lanes, lanes), 0) == lax.broadcasted_iota(jnp.int32, (lanes, lanes), 1)

    @pl.loop(0, extent)
    def _(row):
        block = matrix[row, 0].astype(f32)
        diag[pl.ds(row, 1), :] = jnp.sum(jnp.where(eye, block, 0.0), axis=0, keepdims=True)

    sub_id = lax.broadcasted_iota(jnp.int32, (8, lanes), 0)

    def product(group, vector):
        base = pl.multiple_of(group * 8, 8)
        for i in range(8):
            for k in range(4):
                picked[k, pl.ds(base + i, 1), :] = vector[pl.ds(sub_columns[base + i, k], 1), :]
        left = jnp.concatenate([picked[k, pl.ds(base, 8), :].astype(bf16) for k in range(4)], axis=1)
        total = jnp.zeros((8, lanes), f32)
        for i in range(8):
            blocks = jnp.concatenate([matrix[base + i, k] for k in range(4)], axis=1)
            made = lax.dot_general(left, blocks, contract_last, preferred_element_type=f32)
            total = jnp.where(sub_id == i, made, total)
        return total

    def groups_of(count, body):
        @pl.loop(0, count // 8)
        def _(group):
            body(group, pl.ds(pl.multiple_of(group * 8, 8), 8))

    ext_a[pl.ds(0, owned), :] = own[...]
    take_margin(0, ext_a)
    loads[4].wait()

    def residual_group(group, rows):
        own[rows, :] = rounded(right_side[rows, :] - product(group, ext_a))

    groups_of(owned, residual_group)
    pack(2, own)
    send_margin(2)

    loads[5].wait()
    flat = jnp.concatenate([own[pl.ds(b, 1), :] for b in range(owned)], axis=1)
    flat = jnp.broadcast_to(flat, (8, flat.shape[1])).astype(bf16)
    local_coarse = lax.dot_general(flat, basis[...], contract_last, preferred_element_type=f32)[0:1, :]
    high = rounded(local_coarse)
    middle = rounded(local_coarse - high)
    low = local_coarse - high - middle
    parts = jnp.concatenate([high, middle, low, jnp.zeros((5, low.shape[1]), f32)], axis=0).astype(bf16)

    @pl.loop(0, wide_count)
    def _(block):
        columns = pl.ds(pl.multiple_of(block * coarse_width, coarse_width), coarse_width)
        spread = lax.dot_general(parts, onehot[:, columns], plain, preferred_element_type=f32)
        partial[block] = jnp.sum(spread, axis=0, keepdims=True)

    residual_wide[0]()

    target[pl.ds(0, owned), :] = own[...]
    take_margin(2, target)
    ext_a[...] = target[...] / diag[...]

    def sweep(count, old, new):
        def body(group, rows):
            new[rows, :] = old[rows, :] + (target[rows, :] - product(group, old)) / diag[rows, :]

        groups_of(count, body)

    def total_of(count, me, mine, landed):
        def add(step, total):
            return total + landed[lax.rem(me + step, count)]

        return lax.fori_loop(1, count, add, mine)

    old, new = ext_a, ext_b
    for turn in range(1, SWEEPS):
        sweep(extent if turn < SWEEPS - 1 else owned, old, new)
        old, new = new, old
        if turn == 1:
            residual_wide[1]()
            wide_sum[...] = total_of(wide_count, w, partial[w], wide_in)
            residual_narrow[0]()
        if turn == 2:
            loads[6].wait()
            residual_narrow[1]()
            block_sum = total_of(narrow_count, n, wide_sum[...], narrow_in)
            block_sum = jnp.broadcast_to(block_sum, (8, coarse_width))
            values = lax.dot_general(
                block_sum, inverse[...], contract_last, precision=lax.Precision.HIGHEST, preferred_element_type=f32
            )[0:1, :]
            value_mine[...] = rounded(values)
            value_in[n] = value_mine[...]
            values_narrow[0]()
    update = old

    values_narrow[1]()
    coarse_mine[...] = jnp.concatenate([value_in[i] for i in range(narrow_count)], axis=1)
    coarse_in[w] = coarse_mine[...]
    values_wide[0]()

    ext_c[pl.ds(0, owned), :] = conc[...]
    take_margin(1, ext_c)

    def gather_faces(place, field):
        @pl.loop(0, owned)
        def _(b):
            for f in range(faces):
                place[b, pl.ds(f, 1), :] = field[pl.ds(face_neighbor[f, b], 1), :]

    gather_faces(near_c, ext_c)
    for load in loads[7:]:
        load.wait()

    values_wide[1]()
    coarse = jnp.concatenate([coarse_in[i] for i in range(wide_count)], axis=1)
    coarse = jnp.broadcast_to(coarse, (8, coarse.shape[1])).astype(bf16)
    chosen = lax.dot_general(coarse, onehot[...], contract_last, preferred_element_type=f32).astype(bf16)
    correction = lax.dot_general(chosen, basis[...], plain, preferred_element_type=f32)
    for b in range(owned):
        own[pl.ds(b, 1), :] = correction[0:1, b * lanes : (b + 1) * lanes]
    own[...] = pressure[...] + update[pl.ds(0, owned), :] + own[...]
    pack(3, own)
    send_margin(3)
    pressure_out[...] = own[...]
    target[pl.ds(0, owned), :] = own[...]
    take_margin(3, target)
    gather_faces(near_p, target)

    @pl.loop(0, owned)
    def _(b):
        row = pl.ds(b, 1)
        flux = trans[:, pl.ds(pl.multiple_of(b * lanes, lanes), lanes)] * (own[row, :] - near_p[b])
        outward, inward = jnp.maximum(flux, 0.0), jnp.minimum(flux, 0.0)
        adv[row, :] = jnp.sum(outward * conc[row, :] + inward * near_c[b], axis=0, keepdims=True)
        ext_b[row, :] = jnp.sum(outward, axis=0, keepdims=True)

    cell_rate = (ext_b[pl.ds(0, owned), :] + rate[...]) / volume[...]
    top_mine[...] = jnp.max(cell_rate, axis=0, keepdims=True)
    tops_narrow[0]()
    scaled = (rate[...] * (inject[...] - conc[...]) - adv[...]) / volume[...]

    def top_of(count, me, mine, landed):
        def larger(step, top):
            return jnp.maximum(top, landed[lax.rem(me + step, count)])

        return lax.fori_loop(1, count, larger, mine)

    tops_narrow[1]()
    top_half[...] = top_of(narrow_count, n, top_mine[...], top_narrow)
    tops_wide[0]()
    tops_wide[1]()
    top = top_of(wide_count, w, top_half[...], top_wide)
    time_step = courant / jnp.max(top, axis=1, keepdims=True)
    conc_out[...] = conc[...] + time_step * scaled

    for turn in range(4):
        for position, offset in enumerate(shift_offsets):
            @pl.when(reaches(offset))
            def _():
                margin_copy(turn, position).wait_send()
    for one in (residual_wide, residual_narrow, values_narrow, values_wide, tops_narrow, tops_wide):
        one[2]()


def solution(mesh):
    wide_count, narrow_count = mesh.shape["wide"], mesh.shape["narrow"]

    def local(
        pressure,
        right_side,
        concentration,
        pore_volume,
        well_rate,
        inject_conc,
        transmissibility,
        face_neighbor,
        sub_matrix,
        sub_columns,
        send_blocks,
        send_counts,
        basis_weights,
        coarse_index,
        coarse_inverse,
    ):
        owned, lanes = pressure.shape
        extent = sub_matrix.shape[0]
        slots = send_blocks.shape[-1]
        faces = face_neighbor.shape[0]
        functions = coarse_index.shape[0]
        coarse_rows, coarse_width = coarse_inverse.shape
        coarse_total = coarse_width * wide_count
        streamed = (
            pressure,
            right_side,
            concentration,
            pore_volume,
            well_rate,
            inject_conc,
            transmissibility,
            sub_matrix,
            basis_weights,
            coarse_inverse,
        )
        dma, vmem = pltpu.SemaphoreType.DMA, pltpu.VMEM
        field, ext = vmem((owned, lanes), f32), vmem((extent, lanes), f32)
        out = jax.ShapeDtypeStruct((owned, lanes), f32)
        return pl.pallas_call(
            functools.partial(kernel, wide_count, narrow_count),
            out_shape=(out, out),
            in_specs=[pl.BlockSpec(memory_space=pltpu.SMEM)] * 4
            + [pl.BlockSpec(memory_space=pltpu.VMEM)]
            + [pl.BlockSpec(memory_space=pl.ANY)] * len(streamed),
            out_specs=[pl.BlockSpec(memory_space=pltpu.VMEM)] * 2,
            scratch_shapes=[vmem(value.shape, value.dtype) for value in streamed]
            + [
                dma((11,)),
                vmem((4, 4, slots, lanes), f32),
                vmem((4, 4, slots, lanes), f32),
                dma((4, 4)),
                dma((4, 4)),
                field,
                ext,
                ext,
                ext,
                ext,
                vmem((4, extent, lanes), f32),
                vmem((functions, coarse_total), bf16),
                vmem((wide_count, 1, coarse_width), f32),
                vmem((wide_count, 1, coarse_width), f32),
                vmem((1, coarse_width), f32),
                vmem((narrow_count, 1, coarse_width), f32),
                vmem((narrow_count, 1, coarse_rows), f32),
                vmem((1, coarse_rows), f32),
                vmem((wide_count, 1, coarse_width), f32),
                vmem((1, coarse_width), f32),
                vmem((1, lanes), f32),
                vmem((narrow_count, 1, lanes), f32),
                vmem((1, lanes), f32),
                vmem((wide_count, 1, lanes), f32),
                dma((3, wide_count)),
                dma((3, wide_count)),
                dma((3, narrow_count)),
                dma((3, narrow_count)),
                vmem((owned, faces, lanes), f32),
                vmem((owned, faces, lanes), f32),
                ext,
                field,
            ],
            compiler_params=pltpu.CompilerParams(
                collective_id=0, has_side_effects=True, vmem_limit_bytes=48 << 20
            ),
            name="iteration",
        )(
            face_neighbor,
            sub_columns,
            send_blocks,
            send_counts,
            coarse_index.reshape(functions, 1),
            *streamed,
        )

    split = ("wide", "narrow")
    return jax.shard_map(
        local,
        mesh=mesh,
        in_specs=(
            P(split, None),
            P(split, None),
            P(split, None),
            P(split, None),
            P(split, None),
            P(split, None),
            P(None, split),
            P(None, split),
            P(split, None, None, None),
            P(split, None),
            P(split, None, None),
            P(split, None),
            P(split, None),
            P(split),
            P(split, None),
        ),
        out_specs=(P(split, None), P(split, None)),
        check_vma=False,
    )
```

```python
import functools

import jax
import jax.numpy as jnp
from jax import lax
from jax.experimental import pallas as pl
from jax.experimental.pallas import tpu as pltpu
from jax.sharding import PartitionSpec as P

SWEEPS = 4

shift_offsets = (2, 1, -1, -2)
courant = 0.9
MESH = pl.DeviceIdType.MESH
f32, bf16 = jnp.float32, jnp.bfloat16
contract_last = (((1,), (1,)), ((), ()))
plain = (((1,), (0,)), ((), ()))


def rounded(value):
    return value.astype(bf16).astype(f32)


def kernel(
    wide_count,
    narrow_count,
    face_neighbor,
    sub_columns,
    send_blocks,
    send_counts,
    index_row,
    pressure_hbm,
    right_hbm,
    conc_hbm,
    volume_hbm,
    rate_hbm,
    inject_hbm,
    trans_hbm,
    matrix_hbm,
    basis_hbm,
    inverse_hbm,
    pressure_out,
    conc_out,
    pressure,
    right_side,
    conc,
    volume,
    rate,
    inject,
    trans,
    matrix,
    basis,
    inverse,
    load_sem,
    outbox,
    inbox,
    margin_send,
    margin_recv,
    own,
    ext_a,
    ext_b,
    target,
    diag,
    picked,
    onehot,
    partial,
    residual_in,
    value_in,
    value_mine,
    top_mine,
    top_in,
    all_send,
    all_recv,
    near_p,
    near_c,
    ext_c,
    adv,
):
    w, n = lax.axis_index("wide"), lax.axis_index("narrow")
    devices, me = wide_count * narrow_count, w * narrow_count + n
    owned, lanes = pressure.shape
    extent = ext_a.shape[0]
    slots = outbox.shape[2]
    faces = trans.shape[0]
    coarse_width = inverse.shape[1]

    loads = []
    sources = (
        (pressure_hbm, pressure),
        (conc_hbm, conc),
        (matrix_hbm.at[pl.ds(0, owned)], matrix.at[pl.ds(0, owned)]),
        (matrix_hbm.at[pl.ds(owned, extent - owned)], matrix.at[pl.ds(owned, extent - owned)]),
        (right_hbm, right_side),
        (basis_hbm, basis),
        (inverse_hbm, inverse),
        (trans_hbm, trans),
        (volume_hbm, volume),
        (rate_hbm, rate),
        (inject_hbm, inject),
    )
    for at, (source, place) in enumerate(sources):
        copy = pltpu.make_async_copy(source, place, load_sem.at[at])
        copy.start()
        loads.append(copy)

    barrier = pltpu.get_barrier_semaphore()

    @pl.loop(1, devices)
    def _(step):
        peer = lax.rem(me + step, devices)
        pl.semaphore_signal(barrier, inc=1, device_id=(peer // narrow_count, lax.rem(peer, narrow_count)), device_id_type=MESH)


    def margin_copy(turn, position):
        offset = shift_offsets[position]
        return pltpu.make_async_remote_copy(
            src_ref=outbox.at[turn, position],
            dst_ref=inbox.at[turn, position],
            send_sem=margin_send.at[turn, position],
            recv_sem=margin_recv.at[turn, position],
            device_id=(w + offset, n),
            device_id_type=MESH,
        )

    def reaches(offset):
        return jnp.logical_and(w + offset >= 0, w + offset < wide_count)

    slot_id = lax.broadcasted_iota(jnp.int32, (slots, lanes), 0)

    def pack(turn, rows):
        for position in range(4):
            for t in range(slots):
                outbox[turn, position, pl.ds(t, 1), :] = rows[pl.ds(send_blocks[0, position, t], 1), :]
            filled = outbox[turn, position]
            outbox[turn, position] = jnp.where(slot_id < send_counts[0, position], filled, 0.0)

    def send_margin(turn):
        for position, offset in enumerate(shift_offsets):
            @pl.when(reaches(offset))
            def _():
                margin_copy(turn, position).start()

    def take_margin(turn, place):
        for position, offset in enumerate(shift_offsets):
            rows = pl.ds(owned + position * slots, slots)

            @pl.when(reaches(-offset))
            def _():
                margin_copy(turn, position).wait_recv()
                place[rows, :] = inbox[turn, position]

            @pl.when(jnp.logical_not(reaches(-offset)))
            def _():
                place[rows, :] = jnp.zeros((slots, lanes), f32)

    def exchange(turn, send_from, land_in):
        def describe(peer, slot):
            return pltpu.make_async_remote_copy(
                src_ref=send_from(peer),
                dst_ref=land_in.at[slot],
                send_sem=all_send.at[turn, peer],
                recv_sem=all_recv.at[turn, slot],
                device_id=(peer // narrow_count, lax.rem(peer, narrow_count)),
                device_id_type=MESH,
            )

        def start():
            @pl.loop(1, devices)
            def _(step):
                describe(lax.rem(me + step, devices), me).start()

        def take():
            @pl.loop(1, devices)
            def _(step):
                peer = lax.rem(me + step, devices)
                describe(peer, peer).wait_recv()

        def finish():
            @pl.loop(1, devices)
            def _(step):
                describe(lax.rem(me + step, devices), me).wait_send()

        return start, take, finish

    residuals = exchange(0, lambda peer: partial.at[peer // narrow_count], residual_in)
    values_all = exchange(1, lambda peer: value_mine, value_in)
    tops = exchange(2, lambda peer: top_mine, top_in)

    @pl.loop(0, onehot.shape[0] // lanes)
    def _(chunk):
        numbers = lax.broadcasted_iota(jnp.int32, (lanes, onehot.shape[1]), 0) + chunk * lanes
        hit = jnp.where(index_row[...] == numbers, 1.0, 0.0)
        onehot[pl.ds(pl.multiple_of(chunk * lanes, lanes), lanes), :] = hit.astype(bf16)

    loads[0].wait()
    own[...] = rounded(pressure[...])
    pack(0, own)
    pl.semaphore_wait(barrier, devices - 1)
    send_margin(0)
    loads[1].wait()
    pack(1, conc)
    send_margin(1)

    loads[2].wait()
    loads[3].wait()
    eye = lax.broadcasted_iota(jnp.int32, (lanes, lanes), 0) == lax.broadcasted_iota(jnp.int32, (lanes, lanes), 1)

    @pl.loop(0, extent)
    def _(row):
        block = matrix[row, 0].astype(f32)
        diag[pl.ds(row, 1), :] = jnp.sum(jnp.where(eye, block, 0.0), axis=0, keepdims=True)

    sub_id = lax.broadcasted_iota(jnp.int32, (8, lanes), 0)

    def product(group, vector):
        base = pl.multiple_of(group * 8, 8)
        for i in range(8):
            for k in range(4):
                picked[k, pl.ds(base + i, 1), :] = vector[pl.ds(sub_columns[k, base + i], 1), :]
        left = jnp.concatenate([picked[k, pl.ds(base, 8), :].astype(bf16) for k in range(4)], axis=1)
        total = jnp.zeros((8, lanes), f32)
        for i in range(8):
            blocks = jnp.concatenate([matrix[base + i, k] for k in range(4)], axis=1)
            made = lax.dot_general(left, blocks, contract_last, preferred_element_type=f32)
            total = jnp.where(sub_id == i, made, total)
        return total

    def groups_of(count, body):
        @pl.loop(0, count // 8)
        def _(group):
            body(group, pl.ds(pl.multiple_of(group * 8, 8), 8))

    ext_a[pl.ds(0, owned), :] = own[...]
    take_margin(0, ext_a)
    loads[4].wait()

    def residual_group(group, rows):
        own[rows, :] = rounded(right_side[rows, :] - product(group, ext_a))

    groups_of(owned, residual_group)
    pack(2, own)
    send_margin(2)

    loads[5].wait()
    flat = jnp.concatenate([own[pl.ds(b, 1), :] for b in range(owned)], axis=1)
    flat = jnp.broadcast_to(flat, (8, flat.shape[1])).astype(bf16)
    local_coarse = lax.dot_general(flat, basis[...], contract_last, preferred_element_type=f32)[0:1, :]
    high = rounded(local_coarse)
    middle = rounded(local_coarse - high)
    low = local_coarse - high - middle
    parts = jnp.concatenate([high, middle, low, jnp.zeros((5, low.shape[1]), f32)], axis=0).astype(bf16)

    @pl.loop(0, wide_count)
    def _(block):
        columns = pl.ds(pl.multiple_of(block * coarse_width, coarse_width), coarse_width)
        spread = lax.dot_general(parts, onehot[columns, :], contract_last, preferred_element_type=f32)
        partial[block] = jnp.sum(spread, axis=0, keepdims=True)

    residuals[0]()

    target[pl.ds(0, owned), :] = own[...]
    take_margin(2, target)
    ext_a[...] = target[...] / diag[...]

    def sweep(count, old, new):
        def body(group, rows):
            new[rows, :] = old[rows, :] + (target[rows, :] - product(group, old)) / diag[rows, :]

        groups_of(count, body)

    old, new = ext_a, ext_b
    for turn in range(1, SWEEPS):
        sweep(extent if turn < SWEEPS - 1 else owned, old, new)
        old, new = new, old
        if turn == 2:
            loads[6].wait()
            residual_in[me] = partial[w]
            residuals[1]()
            block_sum = jnp.broadcast_to(jnp.sum(residual_in[...], axis=0), (8, coarse_width))
            values = lax.dot_general(
                block_sum, inverse[...], contract_last, precision=lax.Precision.HIGHEST, preferred_element_type=f32
            )[0:1, :]
            value_mine[...] = rounded(values)
            value_in[me] = value_mine[...]
            values_all[0]()
    update = old

    ext_c[pl.ds(0, owned), :] = conc[...]
    take_margin(1, ext_c)

    def gather_faces(place, field):
        @pl.loop(0, owned)
        def _(b):
            for f in range(faces):
                place[b, pl.ds(f, 1), :] = field[pl.ds(face_neighbor[f, b], 1), :]

    gather_faces(near_c, ext_c)
    for load in loads[7:]:
        load.wait()

    values_all[1]()
    coarse = jnp.concatenate([value_in[i] for i in range(devices)], axis=1)
    coarse = jnp.broadcast_to(coarse, (8, coarse.shape[1])).astype(bf16)
    chosen = lax.dot_general(coarse, onehot[...], plain, preferred_element_type=f32).astype(bf16)
    correction = lax.dot_general(chosen, basis[...], plain, preferred_element_type=f32)
    for b in range(owned):
        own[pl.ds(b, 1), :] = correction[0:1, b * lanes : (b + 1) * lanes]
    own[...] = pressure[...] + update[pl.ds(0, owned), :] + own[...]
    pack(3, own)
    send_margin(3)
    pressure_out[...] = own[...]
    target[pl.ds(0, owned), :] = own[...]
    take_margin(3, target)
    gather_faces(near_p, target)

    @pl.loop(0, owned)
    def _(b):
        row = pl.ds(b, 1)
        flux = trans[:, pl.ds(pl.multiple_of(b * lanes, lanes), lanes)] * (own[row, :] - near_p[b])
        outward, inward = jnp.maximum(flux, 0.0), jnp.minimum(flux, 0.0)
        adv[row, :] = jnp.sum(outward * conc[row, :] + inward * near_c[b], axis=0, keepdims=True)
        ext_b[row, :] = jnp.sum(outward, axis=0, keepdims=True)

    cell_rate = (ext_b[pl.ds(0, owned), :] + rate[...]) / volume[...]
    top_mine[...] = jnp.max(cell_rate, axis=0, keepdims=True)
    tops[0]()
    scaled = (rate[...] * (inject[...] - conc[...]) - adv[...]) / volume[...]

    top_in[me] = top_mine[...]
    tops[1]()
    top = jnp.max(top_in[...], axis=0)
    time_step = courant / jnp.max(top, axis=1, keepdims=True)
    conc_out[...] = conc[...] + time_step * scaled

    for turn in range(4):
        for position, offset in enumerate(shift_offsets):
            @pl.when(reaches(offset))
            def _():
                margin_copy(turn, position).wait_send()
    for one in (residuals, values_all, tops):
        one[2]()


def solution(mesh):
    wide_count, narrow_count = mesh.shape["wide"], mesh.shape["narrow"]

    def local(
        pressure,
        right_side,
        concentration,
        pore_volume,
        well_rate,
        inject_conc,
        transmissibility,
        face_neighbor,
        sub_matrix,
        sub_columns,
        send_blocks,
        send_counts,
        basis_weights,
        coarse_index,
        coarse_inverse,
    ):
        owned, lanes = pressure.shape
        extent = sub_matrix.shape[0]
        slots = send_blocks.shape[-1]
        faces = face_neighbor.shape[0]
        functions = coarse_index.shape[0]
        coarse_rows, coarse_width = coarse_inverse.shape
        coarse_total = coarse_width * wide_count
        devices = wide_count * narrow_count
        streamed = (
            pressure,
            right_side,
            concentration,
            pore_volume,
            well_rate,
            inject_conc,
            transmissibility,
            sub_matrix,
            basis_weights,
            coarse_inverse,
        )
        dma, vmem = pltpu.SemaphoreType.DMA, pltpu.VMEM
        field, ext = vmem((owned, lanes), f32), vmem((extent, lanes), f32)
        out = jax.ShapeDtypeStruct((owned, lanes), f32)
        return pl.pallas_call(
            functools.partial(kernel, wide_count, narrow_count),
            out_shape=(out, out),
            in_specs=[pl.BlockSpec(memory_space=pltpu.SMEM)] * 4
            + [pl.BlockSpec(memory_space=pltpu.VMEM)]
            + [pl.BlockSpec(memory_space=pltpu.HBM)] * len(streamed),
            out_specs=[pl.BlockSpec(memory_space=pltpu.VMEM)] * 2,
            scratch_shapes=[vmem(value.shape, value.dtype) for value in streamed]
            + [
                dma((11,)),
                vmem((4, 4, slots, lanes), f32),
                vmem((4, 4, slots, lanes), f32),
                dma((4, 4)),
                dma((4, 4)),
                field,
                ext,
                ext,
                ext,
                ext,
                vmem((4, extent, lanes), f32),
                vmem((coarse_total, functions), bf16),
                vmem((wide_count, 1, coarse_width), f32),
                vmem((devices, 1, coarse_width), f32),
                vmem((devices, 1, coarse_rows), f32),
                vmem((1, coarse_rows), f32),
                vmem((1, lanes), f32),
                vmem((devices, 1, lanes), f32),
                dma((3, devices)),
                dma((3, devices)),
                vmem((owned, faces, lanes), f32),
                vmem((owned, faces, lanes), f32),
                ext,
                field,
            ],
            compiler_params=pltpu.CompilerParams(
                collective_id=0, has_side_effects=True, vmem_limit_bytes=60 << 20
            ),
            name="iteration",
        )(
            face_neighbor,
            sub_columns.T,
            send_blocks,
            send_counts,
            coarse_index.reshape(1, functions),
            *streamed,
        )

    split = ("wide", "narrow")
    return jax.shard_map(
        local,
        mesh=mesh,
        in_specs=(
            P(split, None),
            P(split, None),
            P(split, None),
            P(split, None),
            P(split, None),
            P(split, None),
            P(None, split),
            P(None, split),
            P(split, None, None, None),
            P(split, None),
            P(split, None, None),
            P(split, None),
            P(split, None),
            P(split),
            P(split, None),
        ),
        out_specs=(P(split, None), P(split, None)),
        check_vma=False,
    )
```

```python
import functools

import jax
import jax.numpy as jnp
from jax import lax
from jax.experimental import pallas as pl
from jax.experimental.pallas import tpu as pltpu
from jax.sharding import PartitionSpec as P

SWEEPS = 4

shift_offsets = (2, 1, -1, -2)
courant = 0.9
MESH = pl.DeviceIdType.MESH
f32, bf16 = jnp.float32, jnp.bfloat16
contract_last = (((1,), (1,)), ((), ()))
plain = (((1,), (0,)), ((), ()))


def rounded(value):
    return value.astype(bf16).astype(f32)


def kernel(
    wide_count,
    narrow_count,
    face_neighbor,
    sub_columns,
    send_blocks,
    send_counts,
    index_row,
    pressure_hbm,
    right_hbm,
    conc_hbm,
    volume_hbm,
    rate_hbm,
    inject_hbm,
    trans_hbm,
    matrix_hbm,
    basis_hbm,
    inverse_hbm,
    pressure_out,
    conc_out,
    pressure,
    right_side,
    conc,
    volume,
    rate,
    inject,
    trans,
    matrix,
    basis,
    inverse,
    load_sem,
    outbox,
    inbox,
    margin_send,
    margin_recv,
    own,
    ext_a,
    ext_b,
    target,
    diag,
    picked,
    onehot,
    partial,
    residual_in,
    value_in,
    value_mine,
    top_mine,
    top_in,
    all_send,
    all_recv,
    near_p,
    near_c,
    ext_c,
    adv,
):
    w, n = lax.axis_index("wide"), lax.axis_index("narrow")
    devices, me = wide_count * narrow_count, w * narrow_count + n
    owned, lanes = pressure.shape
    extent = ext_a.shape[0]
    slots = outbox.shape[2]
    faces = trans.shape[0]
    coarse_width = inverse.shape[1]

    loads = []
    sources = (
        (pressure_hbm, pressure),
        (conc_hbm, conc),
        (matrix_hbm.at[pl.ds(0, owned)], matrix.at[pl.ds(0, owned)]),
        (matrix_hbm.at[pl.ds(owned, extent - owned)], matrix.at[pl.ds(owned, extent - owned)]),
        (right_hbm, right_side),
        (basis_hbm, basis),
        (inverse_hbm, inverse),
        (trans_hbm, trans),
        (volume_hbm, volume),
        (rate_hbm, rate),
        (inject_hbm, inject),
    )
    for at, (source, place) in enumerate(sources):
        copy = pltpu.make_async_copy(source, place, load_sem.at[at])
        copy.start()
        loads.append(copy)

    barrier = pltpu.get_barrier_semaphore()

    def wrapped(at, count):
        return jnp.where(at >= count, at - count, at)

    def each_other(body):
        columns = [n] + [wrapped(n + step, narrow_count) for step in range(1, narrow_count)]
        for column in columns[1:]:
            body(w, column)

        @pl.loop(1, wide_count)
        def _(step):
            row = wrapped(w + step, wide_count)
            for column in columns:
                body(row, column)

    each_other(lambda row, column: pl.semaphore_signal(barrier, inc=1, device_id=(row, column), device_id_type=MESH))

    def margin_copy(turn, position):
        offset = shift_offsets[position]
        return pltpu.make_async_remote_copy(
            src_ref=outbox.at[turn, position],
            dst_ref=inbox.at[turn, position],
            send_sem=margin_send.at[turn, position],
            recv_sem=margin_recv.at[turn, position],
            device_id=(w + offset, n),
            device_id_type=MESH,
        )

    def reaches(offset):
        return jnp.logical_and(w + offset >= 0, w + offset < wide_count)

    slot_id = lax.broadcasted_iota(jnp.int32, (slots, lanes), 0)

    def pack(turn, rows):
        for position in range(4):
            for t in range(slots):
                outbox[turn, position, pl.ds(t, 1), :] = rows[pl.ds(send_blocks[0, position, t], 1), :]
            filled = outbox[turn, position]
            outbox[turn, position] = jnp.where(slot_id < send_counts[0, position], filled, 0.0)

    def send_margin(turn):
        for position, offset in enumerate(shift_offsets):
            @pl.when(reaches(offset))
            def _():
                margin_copy(turn, position).start()

    def take_margin(turn, place):
        for position, offset in enumerate(shift_offsets):
            rows = pl.ds(owned + position * slots, slots)

            @pl.when(reaches(-offset))
            def _():
                margin_copy(turn, position).wait_recv()
                place[rows, :] = inbox[turn, position]

            @pl.when(jnp.logical_not(reaches(-offset)))
            def _():
                place[rows, :] = jnp.zeros((slots, lanes), f32)

    def exchange(turn, send_from, land_in):
        def start():
            def send(row, column):
                pltpu.make_async_remote_copy(
                    src_ref=send_from(row),
                    dst_ref=land_in.at[me],
                    send_sem=all_send.at[turn],
                    recv_sem=all_recv.at[turn],
                    device_id=(row, column),
                    device_id_type=MESH,
                ).start()

            each_other(send)

        others = land_in.at[pl.ds(0, devices - 1)]
        every = pltpu.make_async_remote_copy(
            src_ref=others,
            dst_ref=others,
            send_sem=all_send.at[turn],
            recv_sem=all_recv.at[turn],
            device_id=(wrapped(w + 1, wide_count), n),
            device_id_type=MESH,
        )
        return start, every.wait_recv, every.wait_send

    residuals = exchange(0, lambda row: partial.at[row], residual_in)
    values_all = exchange(1, lambda row: value_mine, value_in)
    tops = exchange(2, lambda row: top_mine, top_in)

    @pl.loop(0, onehot.shape[0] // lanes)
    def _(chunk):
        numbers = lax.broadcasted_iota(jnp.int32, (lanes, onehot.shape[1]), 0) + chunk * lanes
        hit = jnp.where(index_row[...] == numbers, 1.0, 0.0)
        onehot[pl.ds(pl.multiple_of(chunk * lanes, lanes), lanes), :] = hit.astype(bf16)

    loads[0].wait()
    own[...] = rounded(pressure[...])
    pack(0, own)
    pl.semaphore_wait(barrier, devices - 1)
    send_margin(0)
    loads[1].wait()
    pack(1, conc)
    send_margin(1)

    loads[2].wait()
    loads[3].wait()
    eye = lax.broadcasted_iota(jnp.int32, (lanes, lanes), 0) == lax.broadcasted_iota(jnp.int32, (lanes, lanes), 1)

    @pl.loop(0, extent)
    def _(row):
        block = matrix[row, 0].astype(f32)
        diag[pl.ds(row, 1), :] = jnp.sum(jnp.where(eye, block, 0.0), axis=0, keepdims=True)

    sub_id = lax.broadcasted_iota(jnp.int32, (8, lanes), 0)

    def product(group, vector):
        base = pl.multiple_of(group * 8, 8)
        for i in range(8):
            for k in range(4):
                picked[k, pl.ds(base + i, 1), :] = vector[pl.ds(sub_columns[k, base + i], 1), :]
        left = jnp.concatenate([picked[k, pl.ds(base, 8), :].astype(bf16) for k in range(4)], axis=1)
        total = jnp.zeros((8, lanes), f32)
        for i in range(0, 8, 2):
            pair = matrix[pl.ds(base + i, 2)]
            blocks = jnp.concatenate([pair[:, k].reshape(2 * lanes, lanes) for k in range(4)], axis=1)
            made = lax.dot_general(left, blocks, contract_last, preferred_element_type=f32)
            total = jnp.where(sub_id == i, made[:, :lanes], total)
            total = jnp.where(sub_id == i + 1, made[:, lanes:], total)
        return total

    def groups_of(count, body):
        @pl.loop(0, count // 8)
        def _(group):
            body(group, pl.ds(pl.multiple_of(group * 8, 8), 8))

    ext_a[pl.ds(0, owned), :] = own[...]
    take_margin(0, ext_a)
    loads[4].wait()

    def residual_group(group, rows):
        own[rows, :] = rounded(right_side[rows, :] - product(group, ext_a))

    groups_of(owned, residual_group)
    pack(2, own)
    send_margin(2)

    loads[5].wait()
    flat = jnp.concatenate([own[pl.ds(b, 1), :] for b in range(owned)], axis=1)
    flat = jnp.broadcast_to(flat, (8, flat.shape[1])).astype(bf16)
    local_coarse = lax.dot_general(flat, basis[...], contract_last, preferred_element_type=f32)[0:1, :]
    high = rounded(local_coarse)
    middle = rounded(local_coarse - high)
    low = local_coarse - high - middle
    parts = jnp.concatenate([high, middle, low, jnp.zeros((5, low.shape[1]), f32)], axis=0).astype(bf16)

    @pl.loop(0, wide_count)
    def _(block):
        columns = pl.ds(pl.multiple_of(block * coarse_width, coarse_width), coarse_width)
        spread = lax.dot_general(parts, onehot[columns, :], contract_last, preferred_element_type=f32)
        partial[block] = jnp.sum(spread, axis=0, keepdims=True)

    residuals[0]()

    target[pl.ds(0, owned), :] = own[...]
    take_margin(2, target)
    ext_a[...] = target[...] / diag[...]

    def sweep(count, old, new):
        def body(group, rows):
            new[rows, :] = old[rows, :] + (target[rows, :] - product(group, old)) / diag[rows, :]

        groups_of(count, body)

    old, new = ext_a, ext_b
    for turn in range(1, SWEEPS):
        sweep(extent if turn < SWEEPS - 1 else owned, old, new)
        old, new = new, old
        if turn == 2:
            loads[6].wait()
            residual_in[me] = partial[w]
            residuals[1]()
            block_sum = jnp.broadcast_to(jnp.sum(residual_in[...], axis=0), (8, coarse_width))
            values = lax.dot_general(
                block_sum, inverse[...], contract_last, precision=lax.Precision.HIGHEST, preferred_element_type=f32
            )[0:1, :]
            value_mine[...] = rounded(values)
            value_in[me] = value_mine[...]
            values_all[0]()
    update = old

    ext_c[pl.ds(0, owned), :] = conc[...]
    take_margin(1, ext_c)

    def gather_faces(place, field):
        @pl.loop(0, owned)
        def _(b):
            for f in range(faces):
                place[b, pl.ds(f, 1), :] = field[pl.ds(face_neighbor[f, b], 1), :]

    gather_faces(near_c, ext_c)
    for load in loads[7:]:
        load.wait()

    values_all[1]()
    coarse = jnp.concatenate([value_in[i] for i in range(devices)], axis=1)
    coarse = jnp.broadcast_to(coarse, (8, coarse.shape[1])).astype(bf16)
    chosen = lax.dot_general(coarse, onehot[...], plain, preferred_element_type=f32).astype(bf16)
    correction = lax.dot_general(chosen, basis[...], plain, preferred_element_type=f32)
    for b in range(owned):
        own[pl.ds(b, 1), :] = correction[0:1, b * lanes : (b + 1) * lanes]
    own[...] = pressure[...] + update[pl.ds(0, owned), :] + own[...]
    pack(3, own)
    send_margin(3)
    pressure_out[...] = own[...]
    target[pl.ds(0, owned), :] = own[...]
    take_margin(3, target)
    gather_faces(near_p, target)

    @pl.loop(0, owned)
    def _(b):
        row = pl.ds(b, 1)
        flux = trans[:, pl.ds(pl.multiple_of(b * lanes, lanes), lanes)] * (own[row, :] - near_p[b])
        outward, inward = jnp.maximum(flux, 0.0), jnp.minimum(flux, 0.0)
        adv[row, :] = jnp.sum(outward * conc[row, :] + inward * near_c[b], axis=0, keepdims=True)
        ext_b[row, :] = jnp.sum(outward, axis=0, keepdims=True)

    cell_rate = (ext_b[pl.ds(0, owned), :] + rate[...]) / volume[...]
    top_mine[...] = jnp.max(cell_rate, axis=0, keepdims=True)
    tops[0]()
    scaled = (rate[...] * (inject[...] - conc[...]) - adv[...]) / volume[...]

    top_in[me] = top_mine[...]
    tops[1]()
    top = jnp.max(top_in[...], axis=0)
    time_step = courant / jnp.max(top, axis=1, keepdims=True)
    conc_out[...] = conc[...] + time_step * scaled

    for turn in range(4):
        for position, offset in enumerate(shift_offsets):
            @pl.when(reaches(offset))
            def _():
                margin_copy(turn, position).wait_send()
    for one in (residuals, values_all, tops):
        one[2]()


def solution(mesh):
    wide_count, narrow_count = mesh.shape["wide"], mesh.shape["narrow"]

    def local(
        pressure,
        right_side,
        concentration,
        pore_volume,
        well_rate,
        inject_conc,
        transmissibility,
        face_neighbor,
        sub_matrix,
        sub_columns,
        send_blocks,
        send_counts,
        basis_weights,
        coarse_index,
        coarse_inverse,
    ):
        owned, lanes = pressure.shape
        extent = sub_matrix.shape[0]
        slots = send_blocks.shape[-1]
        faces = face_neighbor.shape[0]
        functions = coarse_index.shape[0]
        coarse_rows, coarse_width = coarse_inverse.shape
        coarse_total = coarse_width * wide_count
        devices = wide_count * narrow_count
        streamed = (
            pressure,
            right_side,
            concentration,
            pore_volume,
            well_rate,
            inject_conc,
            transmissibility,
            sub_matrix,
            basis_weights,
            coarse_inverse,
        )
        dma, vmem = pltpu.SemaphoreType.DMA, pltpu.VMEM
        field, ext = vmem((owned, lanes), f32), vmem((extent, lanes), f32)
        out = jax.ShapeDtypeStruct((owned, lanes), f32)
        return pl.pallas_call(
            functools.partial(kernel, wide_count, narrow_count),
            out_shape=(out, out),
            in_specs=[pl.BlockSpec(memory_space=pltpu.SMEM)] * 4
            + [pl.BlockSpec(memory_space=pltpu.VMEM)]
            + [pl.BlockSpec(memory_space=pltpu.HBM)] * len(streamed),
            out_specs=[pl.BlockSpec(memory_space=pltpu.VMEM)] * 2,
            scratch_shapes=[vmem(value.shape, value.dtype) for value in streamed]
            + [
                dma((11,)),
                vmem((4, 4, slots, lanes), f32),
                vmem((4, 4, slots, lanes), f32),
                dma((4, 4)),
                dma((4, 4)),
                field,
                ext,
                ext,
                ext,
                ext,
                vmem((4, extent, lanes), f32),
                vmem((coarse_total, functions), bf16),
                vmem((wide_count, 1, coarse_width), f32),
                vmem((devices, 1, coarse_width), f32),
                vmem((devices, 1, coarse_rows), f32),
                vmem((1, coarse_rows), f32),
                vmem((1, lanes), f32),
                vmem((devices, 1, lanes), f32),
                dma((3,)),
                dma((3,)),
                vmem((owned, faces, lanes), f32),
                vmem((owned, faces, lanes), f32),
                ext,
                field,
            ],
            compiler_params=pltpu.CompilerParams(
                collective_id=0, has_side_effects=True, vmem_limit_bytes=60 << 20
            ),
            name="iteration",
        )(
            face_neighbor,
            sub_columns.T,
            send_blocks,
            send_counts,
            coarse_index.reshape(1, functions),
            *streamed,
        )

    split = ("wide", "narrow")
    return jax.shard_map(
        local,
        mesh=mesh,
        in_specs=(
            P(split, None),
            P(split, None),
            P(split, None),
            P(split, None),
            P(split, None),
            P(split, None),
            P(None, split),
            P(None, split),
            P(split, None, None, None),
            P(split, None),
            P(split, None, None),
            P(split, None),
            P(split, None),
            P(split),
            P(split, None),
        ),
        out_specs=(P(split, None), P(split, None)),
        check_vma=False,
    )
```

```python
import functools

import jax
import jax.numpy as jnp
from jax import lax
from jax.experimental import pallas as pl
from jax.experimental.pallas import tpu as pltpu
from jax.sharding import PartitionSpec as P

SWEEPS = 4

shift_offsets = (2, 1, -1, -2)
courant = 0.9
MESH = pl.DeviceIdType.MESH
f32, bf16 = jnp.float32, jnp.bfloat16
contract_last = (((1,), (1,)), ((), ()))
plain = (((1,), (0,)), ((), ()))


def rounded(value):
    return value.astype(bf16).astype(f32)


def kernel(
    wide_count,
    narrow_count,
    face_neighbor,
    sub_columns,
    send_blocks,
    send_counts,
    index_row,
    pressure_hbm,
    right_hbm,
    conc_hbm,
    volume_hbm,
    rate_hbm,
    inject_hbm,
    trans_hbm,
    matrix_hbm,
    basis_hbm,
    inverse_hbm,
    pressure_out,
    conc_out,
    pressure,
    right_side,
    conc,
    volume,
    rate,
    inject,
    trans,
    matrix,
    basis,
    inverse,
    load_sem,
    outbox,
    inbox,
    margin_send,
    margin_recv,
    own,
    ext_a,
    ext_b,
    target,
    diag,
    picked,
    onehot,
    partial,
    residual_in,
    value_in,
    value_mine,
    top_mine,
    top_in,
    all_send,
    all_recv,
    near_p,
    near_c,
    ext_c,
    adv,
):
    w, n = lax.axis_index("wide"), lax.axis_index("narrow")
    devices, me = wide_count * narrow_count, w * narrow_count + n
    owned, lanes = pressure.shape
    extent = ext_a.shape[0]
    slots = outbox.shape[2]
    faces = trans.shape[0]
    coarse_width = inverse.shape[1]

    loads = []
    sources = (
        (pressure_hbm, pressure),
        (conc_hbm, conc),
        (matrix_hbm.at[pl.ds(0, owned)], matrix.at[pl.ds(0, owned)]),
        (matrix_hbm.at[pl.ds(owned, extent - owned)], matrix.at[pl.ds(owned, extent - owned)]),
        (right_hbm, right_side),
        (basis_hbm, basis),
        (inverse_hbm, inverse),
        (trans_hbm, trans),
        (volume_hbm, volume),
        (rate_hbm, rate),
        (inject_hbm, inject),
    )
    for at, (source, place) in enumerate(sources):
        copy = pltpu.make_async_copy(source, place, load_sem.at[at])
        copy.start()
        loads.append(copy)

    barrier = pltpu.get_barrier_semaphore()

    def wrapped(at, count):
        return jnp.where(at >= count, at - count, at)

    def each_other(body):
        columns = [n] + [wrapped(n + step, narrow_count) for step in range(1, narrow_count)]
        for column in columns[1:]:
            body(w, column)

        @pl.loop(1, wide_count)
        def _(step):
            row = wrapped(w + step, wide_count)
            for column in columns:
                body(row, column)

    each_other(lambda row, column: pl.semaphore_signal(barrier, inc=1, device_id=(row, column), device_id_type=MESH))

    def margin_copy(turn, position):
        offset = shift_offsets[position]
        return pltpu.make_async_remote_copy(
            src_ref=outbox.at[turn, position],
            dst_ref=inbox.at[turn, position],
            send_sem=margin_send.at[turn, position],
            recv_sem=margin_recv.at[turn, position],
            device_id=(w + offset, n),
            device_id_type=MESH,
        )

    def reaches(offset):
        return jnp.logical_and(w + offset >= 0, w + offset < wide_count)

    slot_id = lax.broadcasted_iota(jnp.int32, (slots, lanes), 0)

    def pack(turn, rows):
        for position in range(4):
            for t in range(slots):
                outbox[turn, position, pl.ds(t, 1), :] = rows[pl.ds(send_blocks[0, position, t], 1), :]
            filled = outbox[turn, position]
            outbox[turn, position] = jnp.where(slot_id < send_counts[0, position], filled, 0.0)

    def send_margin(turn):
        for position, offset in enumerate(shift_offsets):
            @pl.when(reaches(offset))
            def _():
                margin_copy(turn, position).start()

    def take_margin(turn, place):
        for position, offset in enumerate(shift_offsets):
            rows = pl.ds(owned + position * slots, slots)

            @pl.when(reaches(-offset))
            def _():
                margin_copy(turn, position).wait_recv()
                place[rows, :] = inbox[turn, position]

            @pl.when(jnp.logical_not(reaches(-offset)))
            def _():
                place[rows, :] = jnp.zeros((slots, lanes), f32)

    def exchange(turn, send_from, land_in):
        def start():
            def send(row, column):
                pltpu.make_async_remote_copy(
                    src_ref=send_from(row),
                    dst_ref=land_in.at[me],
                    send_sem=all_send.at[turn],
                    recv_sem=all_recv.at[turn],
                    device_id=(row, column),
                    device_id_type=MESH,
                ).start()

            each_other(send)

        others = land_in.at[pl.ds(0, devices - 1)]
        every = pltpu.make_async_remote_copy(
            src_ref=others,
            dst_ref=others,
            send_sem=all_send.at[turn],
            recv_sem=all_recv.at[turn],
            device_id=(wrapped(w + 1, wide_count), n),
            device_id_type=MESH,
        )
        return start, every.wait_recv, every.wait_send

    residuals = exchange(0, lambda row: partial.at[row], residual_in)
    values_all = exchange(1, lambda row: value_mine, value_in)
    tops = exchange(2, lambda row: top_mine, top_in)

    @pl.loop(0, onehot.shape[0] // lanes, unroll=2)
    def _(chunk):
        numbers = lax.broadcasted_iota(jnp.int32, (lanes, onehot.shape[1]), 0) + chunk * lanes
        hit = jnp.where(index_row[...] == numbers, 1.0, 0.0)
        onehot[pl.ds(pl.multiple_of(chunk * lanes, lanes), lanes), :] = hit.astype(bf16)

    loads[0].wait()
    own[...] = rounded(pressure[...])
    pack(0, own)
    pl.semaphore_wait(barrier, devices - 1)
    send_margin(0)
    loads[1].wait()
    pack(1, conc)
    send_margin(1)

    loads[2].wait()
    loads[3].wait()
    eye = lax.broadcasted_iota(jnp.int32, (lanes, lanes), 0) == lax.broadcasted_iota(jnp.int32, (lanes, lanes), 1)

    @pl.loop(0, extent, unroll=4)
    def _(row):
        block = matrix[row, 0].astype(f32)
        diag[pl.ds(row, 1), :] = jnp.sum(jnp.where(eye, block, 0.0), axis=0, keepdims=True)

    sub_id = lax.broadcasted_iota(jnp.int32, (8, lanes), 0)

    def product(group, vector):
        base = pl.multiple_of(group * 8, 8)
        for i in range(8):
            for k in range(4):
                picked[k, pl.ds(base + i, 1), :] = vector[pl.ds(sub_columns[k, base + i], 1), :]
        left = jnp.concatenate([picked[k, pl.ds(base, 8), :].astype(bf16) for k in range(4)], axis=1)
        total = jnp.zeros((8, lanes), f32)
        for i in range(0, 8, 2):
            pair = matrix[pl.ds(base + i, 2)]
            blocks = jnp.concatenate([pair[:, k].reshape(2 * lanes, lanes) for k in range(4)], axis=1)
            made = lax.dot_general(left, blocks, contract_last, preferred_element_type=f32)
            total = jnp.where(sub_id == i, made[:, :lanes], total)
            total = jnp.where(sub_id == i + 1, made[:, lanes:], total)
        return total

    def groups_of(count, body):
        @pl.loop(0, count // 8, unroll=2)
        def _(group):
            body(group, pl.ds(pl.multiple_of(group * 8, 8), 8))

    ext_a[pl.ds(0, owned), :] = own[...]
    take_margin(0, ext_a)
    loads[4].wait()

    def residual_group(group, rows):
        own[rows, :] = rounded(right_side[rows, :] - product(group, ext_a))

    groups_of(owned, residual_group)
    pack(2, own)
    send_margin(2)

    loads[5].wait()
    flat = jnp.concatenate([own[pl.ds(b, 1), :] for b in range(owned)], axis=1)
    flat = jnp.broadcast_to(flat, (8, flat.shape[1])).astype(bf16)
    local_coarse = lax.dot_general(flat, basis[...], contract_last, preferred_element_type=f32)[0:1, :]
    high = rounded(local_coarse)
    middle = rounded(local_coarse - high)
    low = local_coarse - high - middle
    parts = jnp.concatenate([high, middle, low, jnp.zeros((5, low.shape[1]), f32)], axis=0).astype(bf16)

    @pl.loop(0, wide_count, unroll=4)
    def _(block):
        columns = pl.ds(pl.multiple_of(block * coarse_width, coarse_width), coarse_width)
        spread = lax.dot_general(parts, onehot[columns, :], contract_last, preferred_element_type=f32)
        partial[block] = jnp.sum(spread, axis=0, keepdims=True)

    residuals[0]()

    target[pl.ds(0, owned), :] = own[...]
    take_margin(2, target)
    ext_a[...] = target[...] / diag[...]

    def sweep(count, old, new):
        def body(group, rows):
            new[rows, :] = old[rows, :] + (target[rows, :] - product(group, old)) / diag[rows, :]

        groups_of(count, body)

    old, new = ext_a, ext_b
    for turn in range(1, SWEEPS):
        sweep(extent if turn < SWEEPS - 1 else owned, old, new)
        old, new = new, old
        if turn == 2:
            loads[6].wait()
            residual_in[me] = partial[w]
            residuals[1]()
            block_sum = jnp.broadcast_to(jnp.sum(residual_in[...], axis=0), (8, coarse_width))
            values = lax.dot_general(
                block_sum, inverse[...], contract_last, precision=lax.Precision.HIGHEST, preferred_element_type=f32
            )[0:1, :]
            value_mine[...] = rounded(values)
            value_in[me] = value_mine[...]
            values_all[0]()
    update = old

    ext_c[pl.ds(0, owned), :] = conc[...]
    take_margin(1, ext_c)

    def gather_faces(place, field):
        @pl.loop(0, owned, unroll=4)
        def _(b):
            for f in range(faces):
                place[b, pl.ds(f, 1), :] = field[pl.ds(face_neighbor[f, b], 1), :]

    gather_faces(near_c, ext_c)
    for load in loads[7:]:
        load.wait()

    values_all[1]()
    coarse = jnp.concatenate([value_in[i] for i in range(devices)], axis=1)
    coarse = jnp.broadcast_to(coarse, (8, coarse.shape[1])).astype(bf16)
    chosen = lax.dot_general(coarse, onehot[...], plain, preferred_element_type=f32).astype(bf16)
    correction = lax.dot_general(chosen, basis[...], plain, preferred_element_type=f32)
    for b in range(owned):
        own[pl.ds(b, 1), :] = correction[0:1, b * lanes : (b + 1) * lanes]
    own[...] = pressure[...] + update[pl.ds(0, owned), :] + own[...]
    pack(3, own)
    send_margin(3)
    pressure_out[...] = own[...]
    target[pl.ds(0, owned), :] = own[...]
    take_margin(3, target)
    gather_faces(near_p, target)

    @pl.loop(0, owned, unroll=4)
    def _(b):
        row = pl.ds(b, 1)
        flux = trans[:, pl.ds(pl.multiple_of(b * lanes, lanes), lanes)] * (own[row, :] - near_p[b])
        outward, inward = jnp.maximum(flux, 0.0), jnp.minimum(flux, 0.0)
        adv[row, :] = jnp.sum(outward * conc[row, :] + inward * near_c[b], axis=0, keepdims=True)
        ext_b[row, :] = jnp.sum(outward, axis=0, keepdims=True)

    cell_rate = (ext_b[pl.ds(0, owned), :] + rate[...]) / volume[...]
    top_mine[...] = jnp.max(cell_rate, axis=0, keepdims=True)
    tops[0]()
    scaled = (rate[...] * (inject[...] - conc[...]) - adv[...]) / volume[...]

    top_in[me] = top_mine[...]
    tops[1]()
    top = jnp.max(top_in[...], axis=0)
    time_step = courant / jnp.max(top, axis=1, keepdims=True)
    conc_out[...] = conc[...] + time_step * scaled

    for turn in range(4):
        for position, offset in enumerate(shift_offsets):
            @pl.when(reaches(offset))
            def _():
                margin_copy(turn, position).wait_send()
    for one in (residuals, values_all, tops):
        one[2]()


def solution(mesh):
    wide_count, narrow_count = mesh.shape["wide"], mesh.shape["narrow"]

    def local(
        pressure,
        right_side,
        concentration,
        pore_volume,
        well_rate,
        inject_conc,
        transmissibility,
        face_neighbor,
        sub_matrix,
        sub_columns,
        send_blocks,
        send_counts,
        basis_weights,
        coarse_index,
        coarse_inverse,
    ):
        owned, lanes = pressure.shape
        extent = sub_matrix.shape[0]
        slots = send_blocks.shape[-1]
        faces = face_neighbor.shape[0]
        functions = coarse_index.shape[0]
        coarse_rows, coarse_width = coarse_inverse.shape
        coarse_total = coarse_width * wide_count
        devices = wide_count * narrow_count
        streamed = (
            pressure,
            right_side,
            concentration,
            pore_volume,
            well_rate,
            inject_conc,
            transmissibility,
            sub_matrix,
            basis_weights,
            coarse_inverse,
        )
        dma, vmem = pltpu.SemaphoreType.DMA, pltpu.VMEM
        field, ext = vmem((owned, lanes), f32), vmem((extent, lanes), f32)
        out = jax.ShapeDtypeStruct((owned, lanes), f32)
        return pl.pallas_call(
            functools.partial(kernel, wide_count, narrow_count),
            out_shape=(out, out),
            in_specs=[pl.BlockSpec(memory_space=pltpu.SMEM)] * 4
            + [pl.BlockSpec(memory_space=pltpu.VMEM)]
            + [pl.BlockSpec(memory_space=pltpu.HBM)] * len(streamed),
            out_specs=[pl.BlockSpec(memory_space=pltpu.VMEM)] * 2,
            scratch_shapes=[vmem(value.shape, value.dtype) for value in streamed]
            + [
                dma((11,)),
                vmem((4, 4, slots, lanes), f32),
                vmem((4, 4, slots, lanes), f32),
                dma((4, 4)),
                dma((4, 4)),
                field,
                ext,
                ext,
                ext,
                ext,
                vmem((4, extent, lanes), f32),
                vmem((coarse_total, functions), bf16),
                vmem((wide_count, 1, coarse_width), f32),
                vmem((devices, 1, coarse_width), f32),
                vmem((devices, 1, coarse_rows), f32),
                vmem((1, coarse_rows), f32),
                vmem((1, lanes), f32),
                vmem((devices, 1, lanes), f32),
                dma((3,)),
                dma((3,)),
                vmem((owned, faces, lanes), f32),
                vmem((owned, faces, lanes), f32),
                ext,
                field,
            ],
            compiler_params=pltpu.CompilerParams(
                collective_id=0, has_side_effects=True, vmem_limit_bytes=60 << 20
            ),
            name="iteration",
        )(
            face_neighbor,
            sub_columns.T,
            send_blocks,
            send_counts,
            coarse_index.reshape(1, functions),
            *streamed,
        )

    split = ("wide", "narrow")
    return jax.shard_map(
        local,
        mesh=mesh,
        in_specs=(
            P(split, None),
            P(split, None),
            P(split, None),
            P(split, None),
            P(split, None),
            P(split, None),
            P(None, split),
            P(None, split),
            P(split, None, None, None),
            P(split, None),
            P(split, None, None),
            P(split, None),
            P(split, None),
            P(split),
            P(split, None),
        ),
        out_specs=(P(split, None), P(split, None)),
        check_vma=False,
    )
```
